32 devices in a mesh: groups: 2 (over x), walker: 16 (over z, y, core).
Axes of the slice: x: 2, y: 2, z: 4, core: 2. Of those that a mesh axis runs over, the one named last changes fastest.
Arguments:
- jacobian_tiles: bfloat16 [32, 192, 2048], P(('groups', 'walker')), parts along dimension 0, may hold values from -6 to 6
Outputs:
- gram: float32 [1536, 768], P(('groups', 'walker')), parts along dimension 0
The draws below stay inside these ranges and needn't reach their ends.
There are 2 independent parts, one for each index of `groups`. The reference program is written for one: setup_inputs(seed, part) draws one part's arguments, and reference() takes and returns one part's arrays. A program takes and returns all parts, laid end to end along the dimension named above; each array names one. Nothing has to cross between parts.
All inputs are finite; a program needn't handle non-finite values.
Results may differ from the reference program's by a relative error of at most 0.0003.
Values may be sent and summed in bfloat16 or wider, within the bound.
No kernel may reach another device: no remote copies, remote signals or barrier semaphores. Data moves between devices by JAX's collectives and lax.ppermute only.
A program may use at most 64 MiB of HBM per device.

```python
import jax
import jax.numpy as jnp

PG = 4
P_SIZE = 8192
W_BLK = 192
CYCLE = 4
PCOL = 2048
WALKERS = 768


def level_of(own_key, dims, pieces, least, high):
    def one(dim, blocks):
        steps = jax.random.uniform(jax.random.fold_in(jax.random.fold_in(own_key, 6), dim), (blocks,), jnp.float32, least / len(pieces), high / len(pieces))
        return jnp.repeat(jnp.exp(steps), dims[dim] // blocks).reshape((-1,) + (1,) * (len(dims) - dim - 1))

    gain = one(*pieces[0])
    for cut in pieces[1:]:
        gain = gain * one(*cut)
    return gain


def normal_values(rng, shape, deviation, bound, shards=(), kind=jnp.bfloat16):
    level = level_of(rng, shape, shards, -0.22, 0.18) if shards else 1.0
    drawn = jax.random.normal(rng, shape, jnp.float32) * deviation * level
    return jnp.minimum(jnp.maximum(drawn, -bound), bound).astype(kind)


def setup_inputs(seed: int = 0, part: int = 0) -> dict:
    keys = jax.random.split(jax.random.key(seed), 2)
    part_keys = jax.random.split(jax.random.fold_in(keys[1], part), 2)
    jacobian_tiles = normal_values(part_keys[0], (CYCLE * PG, W_BLK, PCOL), 1.0, 6.0, ((0, 16),))
    return {"jacobian_tiles": jacobian_tiles}


def reference(jacobian_tiles):
    cycle_len = WALKERS // W_BLK
    jacobian = jacobian_tiles.reshape(cycle_len, PG, W_BLK, PCOL).transpose(0, 2, 1, 3).reshape(WALKERS, P_SIZE)
    return jnp.dot(jacobian, jacobian.T, preferred_element_type=jnp.float32) / P_SIZE
```

```python
import jax
import jax.numpy as jnp
from jax import lax
from jax.sharding import PartitionSpec as P


PG = 4


def dot(a, b):
    return lax.dot_general(a, b, (((1,), (1,)), ((), ())), preferred_element_type=jnp.float32)


def line(jacobian_tiles):
    return body(jacobian_tiles)


def body(jacobian_tiles):
    own = jacobian_tiles[0]
    width, cols = own.shape
    n = lax.axis_size("walker") // PG
    ring = 2 * n
    quarter = width // PG
    me = lax.axis_index("walker")
    pos, group = me // PG, me % PG
    side, core = group // 2, group % 2

    def device(r, y):
        r = r % ring
        return r * PG + 2 * y if r < n else (ring - 1 - r) * PG + 2 * y + 1

    def move(value, step, flip=0, only=None):
        pairs = [
            (device(r, y), device(r + step, y ^ flip))
            for y in range(2)
            for r in range(ring)
            if only is None or r % n in only
        ]
        return lax.ppermute(value, "walker", pairs)

    k = cols // 2
    own_parts = [own[:, :k], own[:, k:]]
    a_parts = [move(part, 1) for part in own_parts]
    b_parts = [move(part, 1, only=(1, 2, 3)) for part in a_parts]
    p = move(own, -1, only=(3,))

    def halves(block):
        block = block.reshape(2, width // 2, width)
        return (
            lax.dynamic_index_in_dim(block, side, 0, False),
            lax.dynamic_index_in_dim(block, 1 - side, 0, False),
        )

    def both(xs, ys):
        return dot(xs[0], ys[0]) + dot(xs[1], ys[1])

    s1 = both(own_parts, own_parts)
    s2 = both(own_parts, a_parts)
    s2t = both(a_parts, own_parts)
    keep, send = zip(*(halves(s) for s in (s1, s2, s2t)))
    early = jnp.stack(keep) + move(jnp.stack(send), 0, 1)
    up1 = move(early[2], -1)

    p_parts = [p[:, :k], p[:, k:]]
    s3 = both(own_parts, b_parts)
    s3t = both(b_parts, own_parts)
    s4 = both(b_parts, p_parts)
    s4t = both(p_parts, b_parts)
    s3k, s3s = halves(s3)
    down2 = s3k + move(s3s, 0, 1)
    tk, ts = halves(s3t)
    up2 = move(tk, -2) + move(ts, -2, 1)
    fk, fs = halves(s4)
    up3 = move(fk, -2, only=(2,)) + move(fs, -2, 1, only=(2,))
    gk, gs = halves(s4t)
    down3 = move(gk, 1, only=(2,)) + move(gs, 1, 1, only=(2,))
    found = {0: early[0], -1: early[1], 1: up1, -2: down2, 2: up2, -3: down3, 3: up3}
    sign = 1 - 2 * core
    blocks = []
    for b in range(n):
        offset = sign * (b - pos)
        value = found[0]
        for d, v in found.items():
            if d:
                value = jnp.where(offset == d, v, value)
        blocks.append(value)
    rows = jnp.stack(blocks, 1).reshape(2, quarter, n * width)
    mine = lax.dynamic_index_in_dim(rows, core, 0, False)
    theirs = lax.dynamic_index_in_dim(rows, 1 - core, 0, False)
    pairs = [(i, i ^ 1) for i in range(n * PG)]
    return (mine + lax.ppermute(theirs, "walker", pairs)) / (cols * PG)


def from_behind(block, axis, distance):
    devices = range(lax.axis_size(axis))
    route = [((i - distance) % len(devices), i) for i in devices]
    return lax.ppermute(block, axis, route)


def from_partner(value, axis, bit):
    mask = 2**bit
    pairs = [(source, source ^ mask) for source in range(lax.axis_size(axis))]
    return lax.ppermute(value, axis, pairs)


def long_line(jacobian_tiles):
    local_block = jacobian_tiles[0]
    blk_width = local_block.shape[0]
    params_all = local_block.shape[1] * PG
    cycle_len = lax.axis_size("walker") // PG
    my_index = lax.axis_index("walker")
    cycle_pos = my_index // PG
    my_group = my_index % PG
    quarter = blk_width // PG

    def tile_with(moving):
        return lax.dot_general(
            local_block, moving, (((1,), (1,)), ((), ())), preferred_element_type=jnp.float32
        )

    stack_init = jnp.zeros((cycle_len, blk_width, blk_width), jnp.float32)
    stack_init = lax.dynamic_update_index_in_dim(stack_init, tile_with(local_block), 0, 0)

    def advance(step_num, carried):
        moving, tile_stack = carried
        moving = from_behind(moving, "walker", -PG)
        tile_stack = lax.dynamic_update_index_in_dim(tile_stack, tile_with(moving), step_num, 0)
        return (moving, tile_stack)

    _, row_stack = lax.fori_loop(1, cycle_len, advance, (local_block, stack_init))
    for bit_num in range(PG.bit_length() - 2, -1, -1):
        half_rows = row_stack.shape[1] // 2
        my_bit = my_group >> bit_num & 1
        kept_rows = lax.dynamic_slice_in_dim(row_stack, my_bit * half_rows, half_rows, 1)
        sent_rows = lax.dynamic_slice_in_dim(row_stack, (1 - my_bit) * half_rows, half_rows, 1)
        row_stack = kept_rows + from_partner(sent_rows, "walker", bit_num)
    row_stack = jnp.roll(row_stack, cycle_pos, axis=0)
    gram_rows = jnp.transpose(row_stack, (1, 0, 2)).reshape(quarter, cycle_len * blk_width)
    return gram_rows / params_all


SPAN = 4


def solution(mesh):
    meets = mesh.shape["walker"] == SPAN * PG
    return jax.shard_map(
        line if meets else long_line,
        mesh=mesh,
        in_specs=(P(("groups", "walker"), None, None),),
        out_specs=P(("groups", "walker"), None),
        check_vma=False,
    )
```

```python
import jax
import jax.numpy as jnp
from jax import lax
from jax.sharding import PartitionSpec as P


PG = 4


def dot(a, b):
    return lax.dot_general(a, b, (((1,), (1,)), ((), ())), preferred_element_type=jnp.float32)


def line(jacobian_tiles):
    return body(jacobian_tiles)


def body(jacobian_tiles):
    own = jacobian_tiles[0]
    width, cols = own.shape
    n = lax.axis_size("walker") // PG
    ring = 2 * n
    quarter = width // PG
    me = lax.axis_index("walker")
    pos, group = me // PG, me % PG
    side, core = group // 2, group % 2
    group_index = jnp.where(core == 0, pos, n - 1 - pos)

    def device(r, y):
        r = r % ring
        return r * PG + 2 * y if r < n else (ring - 1 - r) * PG + 2 * y + 1

    def turn(to, flip=0, keep=lambda q: True):
        return [
            (device(r, y), device(to(r, r % n), y ^ flip))
            for y in range(2)
            for r in range(ring)
            if keep(r % n)
        ]

    def move(value, pairs):
        return lax.ppermute(value, "walker", pairs)

    def pack(value):
        return jnp.concatenate([value[:quarter], value[quarter:]], 1)

    def unpack(value):
        return jnp.concatenate([value[:, :width], value[:, width:]], 0)

    def swap(value):
        pairs = [(i, i ^ 1) for i in range(n * PG)]
        return lax.ppermute(value, "walker", pairs)

    k = cols // 2
    own_parts = [own[:, :k], lax.optimization_barrier(own)[:, k:]]
    a_parts = [move(part, turn(lambda r, q: r + 1)) for part in own_parts]
    b_parts = [move(part, turn(lambda r, q: r + 1)) for part in a_parts]
    p_parts = [swap(part) for part in b_parts]

    def halves(block):
        block = block.reshape(2, width // 2, width)
        return (
            lax.dynamic_index_in_dim(block, side, 0, False),
            lax.dynamic_index_in_dim(block, 1 - side, 0, False),
        )

    s1 = dot(own, own)
    s2, s2t = dot(own_parts[0], a_parts[0]), dot(a_parts[0], own_parts[0])
    s2, s2t = lax.optimization_barrier((s2, s2t))
    s2 += dot(own_parts[1], a_parts[1])
    s2t += dot(a_parts[1], own_parts[1])
    keep, send = zip(*(halves(s) for s in (s1, s2, s2t)))
    early = jnp.stack(keep) + move(jnp.stack(send), turn(lambda r, q: r, 1))
    early = lax.optimization_barrier(early)
    up1 = move(early[2], turn(lambda r, q: r - 1))

    s3, s3t = dot(own_parts[0], b_parts[0]), dot(b_parts[0], own_parts[0])
    s3, s3t = lax.optimization_barrier((s3, s3t))
    s3 += dot(own_parts[1], b_parts[1])
    s3t += dot(b_parts[1], own_parts[1])
    s4, s4t = dot(p_parts[0], b_parts[0]), dot(b_parts[0], p_parts[0])
    s4, s4t = lax.optimization_barrier((s4, s4t))
    s4 += dot(p_parts[1], b_parts[1])
    s4t += dot(b_parts[1], p_parts[1])
    lone = group_index == 1
    far = jnp.where(lone, s4, s3t)
    near = jnp.where(lone, s4t, s3)
    far_keep, far_send = halves(far)
    near_keep, near_send = halves(near)

    route = {0: 6, 1: 3, 2: 0, 3: 1, 4: 2, 5: 7, 6: 4, 7: 5}
    beside = {0: 1, 1: 0, 4: 5, 5: 4}
    x = move(pack(far_keep), turn(lambda r, q: route[r]))
    xf = move(pack(far_send), turn(lambda r, q: route[r], 1))
    y = move(near_send, turn(lambda r, q: beside.get(r, r), 1))
    z = move(near_keep, turn(lambda r, q: beside[r], keep=lambda q: q < 2))
    x, xf, y, z, up1 = lax.optimization_barrier((x, xf, y, z, up1))
    x = unpack(x + xf)
    found = {0: early[0], -1: early[1], 1: up1, 2: x, -3: x, -2: near_keep + y, 3: z + y}
    sign = 1 - 2 * core

    def quarter_of(which):
        blocks = []
        for b in range(n):
            offset = sign * (b - pos)
            value = None
            for d, v in found.items():
                v = lax.dynamic_slice_in_dim(v, which * quarter, quarter, 0)
                value = v if value is None else jnp.where(offset == d, v, value)
            blocks.append(value)
        return jnp.stack(blocks)

    total = quarter_of(core) + swap(quarter_of(1 - core))
    return jnp.concatenate([total[b] for b in range(n)], 1) / (cols * PG)


def from_behind(block, axis, distance):
    devices = range(lax.axis_size(axis))
    route = [((i - distance) % len(devices), i) for i in devices]
    return lax.ppermute(block, axis, route)


def from_partner(value, axis, bit):
    mask = 2**bit
    pairs = [(source, source ^ mask) for source in range(lax.axis_size(axis))]
    return lax.ppermute(value, axis, pairs)


def long_line(jacobian_tiles):
    local_block = jacobian_tiles[0]
    blk_width = local_block.shape[0]
    params_all = local_block.shape[1] * PG
    cycle_len = lax.axis_size("walker") // PG
    my_index = lax.axis_index("walker")
    cycle_pos = my_index // PG
    my_group = my_index % PG
    quarter = blk_width // PG

    def tile_with(moving):
        return lax.dot_general(
            local_block, moving, (((1,), (1,)), ((), ())), preferred_element_type=jnp.float32
        )

    stack_init = jnp.zeros((cycle_len, blk_width, blk_width), jnp.float32)
    stack_init = lax.dynamic_update_index_in_dim(stack_init, tile_with(local_block), 0, 0)

    def advance(step_num, carried):
        moving, tile_stack = carried
        moving = from_behind(moving, "walker", -PG)
        tile_stack = lax.dynamic_update_index_in_dim(tile_stack, tile_with(moving), step_num, 0)
        return (moving, tile_stack)

    _, row_stack = lax.fori_loop(1, cycle_len, advance, (local_block, stack_init))
    for bit_num in range(PG.bit_length() - 2, -1, -1):
        half_rows = row_stack.shape[1] // 2
        my_bit = my_group >> bit_num & 1
        kept_rows = lax.dynamic_slice_in_dim(row_stack, my_bit * half_rows, half_rows, 1)
        sent_rows = lax.dynamic_slice_in_dim(row_stack, (1 - my_bit) * half_rows, half_rows, 1)
        row_stack = kept_rows + from_partner(sent_rows, "walker", bit_num)
    row_stack = jnp.roll(row_stack, cycle_pos, axis=0)
    gram_rows = jnp.transpose(row_stack, (1, 0, 2)).reshape(quarter, cycle_len * blk_width)
    return gram_rows / params_all


SPAN = 4


def solution(mesh):
    meets = mesh.shape["walker"] == SPAN * PG
    return jax.shard_map(
        line if meets else long_line,
        mesh=mesh,
        in_specs=(P(("groups", "walker"), None, None),),
        out_specs=P(("groups", "walker"), None),
        check_vma=False,
    )
```

```python
import jax
import jax.numpy as jnp
from jax import lax
from jax.sharding import PartitionSpec as P


PG = 4


def dot(a, b):
    return lax.dot_general(a, b, (((1,), (1,)), ((), ())), preferred_element_type=jnp.float32)


def line(jacobian_tiles):
    return body(jacobian_tiles)


def body(jacobian_tiles):
    own = jacobian_tiles[0]
    width, cols = own.shape
    n = lax.axis_size("walker") // PG
    ring = 2 * n
    quarter = width // PG
    me = lax.axis_index("walker")
    pos, group = me // PG, me % PG
    side, core = group // 2, group % 2
    group_index = jnp.where(core == 0, pos, n - 1 - pos)

    def device(r, y):
        r = r % ring
        return r * PG + 2 * y if r < n else (ring - 1 - r) * PG + 2 * y + 1

    def turn(to, flip=0, keep=lambda q: True):
        return [
            (device(r, y), device(to(r, r % n), y ^ flip))
            for y in range(2)
            for r in range(ring)
            if keep(r % n)
        ]

    def move(value, pairs):
        return lax.ppermute(value, "walker", pairs)

    def pack(value):
        return jnp.concatenate([value[:quarter], value[quarter:]], 1)

    def unpack(value):
        return jnp.concatenate([value[:, :width], value[:, width:]], 0)

    def swap(value):
        pairs = [(i, i ^ 1) for i in range(n * PG)]
        return lax.ppermute(value, "walker", pairs)

    edges = [cols * c // CUTS[-1] for c in (0, *CUTS)]
    spans = list(zip(edges, edges[1:]))
    own_parts = [own[:, spans[0][0] : spans[0][1]]]
    rest = lax.optimization_barrier(own)
    own_parts += [rest[:, lo:hi] for lo, hi in spans[1:]]
    a_parts = [move(part, turn(lambda r, q: r + 1)) for part in own_parts]
    b_parts = [move(part, turn(lambda r, q: r + 1)) for part in a_parts]
    p_parts = [swap(part) for part in b_parts]

    def products(xs, ys):
        forth, back = 0.0, 0.0
        for i, (x, y) in enumerate(zip(xs, ys)):
            forth += dot(x, y)
            back += dot(y, x)
            if i + 1 < len(xs):
                forth, back = lax.optimization_barrier((forth, back))
        return forth, back

    def halves(block):
        block = block.reshape(2, width // 2, width)
        return (
            lax.dynamic_index_in_dim(block, side, 0, False),
            lax.dynamic_index_in_dim(block, 1 - side, 0, False),
        )

    s1 = dot(own, own)
    s2, s2t = products(own_parts, a_parts)
    keep, send = zip(*(halves(s) for s in (s1, s2, s2t)))
    early = jnp.stack(keep) + move(jnp.stack(send), turn(lambda r, q: r, 1))
    early = lax.optimization_barrier(early)

    s3, s3t = products(own_parts, b_parts)
    s4, s4t = products(p_parts, b_parts)
    lone = group_index == 1
    far = jnp.where(lone, s4, s3t)
    near = jnp.where(lone, s4t, s3)
    far_keep, far_send = halves(far)
    near_keep, near_send = halves(near)

    route = {0: 6, 1: 3, 2: 0, 3: 1, 4: 2, 5: 7, 6: 4, 7: 5}
    beside = {0: 1, 1: 0, 4: 5, 5: 4}
    x = move(pack(far_keep), turn(lambda r, q: route[r]))
    xf = move(pack(far_send), turn(lambda r, q: route[r], 1))
    y = move(pack(near_send), turn(lambda r, q: beside.get(r, r), 1))
    ez = move(jnp.concatenate([early[2], near_keep], 1), turn(lambda r, q: r - 1))
    x, xf, y, ez = lax.optimization_barrier((x, xf, y, ez))
    x = unpack(x + xf)
    y = unpack(y)
    up1, z = ez[:, :width], ez[:, width:]
    found = {0: early[0], -1: early[1], 1: up1, 2: x, -3: x, -2: near_keep + y, 3: z + y}
    sign = 1 - 2 * core

    def quarter_of(which):
        blocks = []
        for b in range(n):
            offset = sign * (b - pos)
            value = None
            for d, v in found.items():
                v = lax.dynamic_slice_in_dim(v, which * quarter, quarter, 0)
                value = v if value is None else jnp.where(offset == d, v, value)
            blocks.append(value)
        return jnp.stack(blocks)

    total = quarter_of(core) + swap(quarter_of(1 - core))
    return jnp.concatenate([total[b] for b in range(n)], 1) / (cols * PG)


def from_behind(block, axis, distance):
    devices = range(lax.axis_size(axis))
    route = [((i - distance) % len(devices), i) for i in devices]
    return lax.ppermute(block, axis, route)


def from_partner(value, axis, bit):
    mask = 2**bit
    pairs = [(source, source ^ mask) for source in range(lax.axis_size(axis))]
    return lax.ppermute(value, axis, pairs)


def long_line(jacobian_tiles):
    local_block = jacobian_tiles[0]
    blk_width = local_block.shape[0]
    params_all = local_block.shape[1] * PG
    cycle_len = lax.axis_size("walker") // PG
    my_index = lax.axis_index("walker")
    cycle_pos = my_index // PG
    my_group = my_index % PG
    quarter = blk_width // PG

    def tile_with(moving):
        return lax.dot_general(
            local_block, moving, (((1,), (1,)), ((), ())), preferred_element_type=jnp.float32
        )

    stack_init = jnp.zeros((cycle_len, blk_width, blk_width), jnp.float32)
    stack_init = lax.dynamic_update_index_in_dim(stack_init, tile_with(local_block), 0, 0)

    def advance(step_num, carried):
        moving, tile_stack = carried
        moving = from_behind(moving, "walker", -PG)
        tile_stack = lax.dynamic_update_index_in_dim(tile_stack, tile_with(moving), step_num, 0)
        return (moving, tile_stack)

    _, row_stack = lax.fori_loop(1, cycle_len, advance, (local_block, stack_init))
    for bit_num in range(PG.bit_length() - 2, -1, -1):
        half_rows = row_stack.shape[1] // 2
        my_bit = my_group >> bit_num & 1
        kept_rows = lax.dynamic_slice_in_dim(row_stack, my_bit * half_rows, half_rows, 1)
        sent_rows = lax.dynamic_slice_in_dim(row_stack, (1 - my_bit) * half_rows, half_rows, 1)
        row_stack = kept_rows + from_partner(sent_rows, "walker", bit_num)
    row_stack = jnp.roll(row_stack, cycle_pos, axis=0)
    gram_rows = jnp.transpose(row_stack, (1, 0, 2)).reshape(quarter, cycle_len * blk_width)
    return gram_rows / params_all


SPAN = 4
CUTS = (3, 6, 8)


def solution(mesh):
    meets = mesh.shape["walker"] == SPAN * PG
    return jax.shard_map(
        line if meets else long_line,
        mesh=mesh,
        in_specs=(P(("groups", "walker"), None, None),),
        out_specs=P(("groups", "walker"), None),
        check_vma=False,
    )
```

```python
import jax
import jax.numpy as jnp
from jax import lax
from jax.sharding import PartitionSpec as P


PG = 4


def dot(a, b):
    return lax.dot_general(a, b, (((1,), (1,)), ((), ())), preferred_element_type=jnp.float32)


def line(jacobian_tiles):
    return body(jacobian_tiles)


def body(jacobian_tiles):
    own = jacobian_tiles[0]
    width, cols = own.shape
    n = lax.axis_size("walker") // PG
    ring = 2 * n
    quarter = width // PG
    me = lax.axis_index("walker")
    pos, group = me // PG, me % PG
    side, core = group // 2, group % 2
    group_index = jnp.where(core == 0, pos, n - 1 - pos)

    def device(r, y):
        r = r % ring
        return r * PG + 2 * y if r < n else (ring - 1 - r) * PG + 2 * y + 1

    def turn(to, flip=0, keep=lambda q: True):
        return [
            (device(r, y), device(to(r, r % n), y ^ flip))
            for y in range(2)
            for r in range(ring)
            if keep(r % n)
        ]

    def move(value, pairs):
        return lax.ppermute(value, "walker", pairs)

    def pack(value):
        return jnp.concatenate([value[:quarter], value[quarter:]], 1)

    def swap(value):
        pairs = [(i, i ^ 1) for i in range(n * PG)]
        return lax.ppermute(value, "walker", pairs)

    edges = [cols * c // CUTS[-1] for c in (0, *CUTS)]
    spans = list(zip(edges, edges[1:]))
    own_parts = [own[:, spans[0][0] : spans[0][1]]]
    rest = lax.optimization_barrier(own)
    own_parts += [rest[:, lo:hi] for lo, hi in spans[1:]]
    a_parts = [move(part, turn(lambda r, q: r + 1)) for part in own_parts]
    b_parts = [move(part, turn(lambda r, q: r + 1)) for part in a_parts]
    p_parts = [swap(part) for part in b_parts]

    def products(xs, ys):
        forth, back = 0.0, 0.0
        for i, (x, y) in enumerate(zip(xs, ys)):
            forth += dot(x, y)
            back += dot(y, x)
            if i + 1 < len(xs):
                forth, back = lax.optimization_barrier((forth, back))
        return forth, back

    def halves(block):
        block = block.reshape(2, width // 2, width)
        return (
            lax.dynamic_index_in_dim(block, side, 0, False),
            lax.dynamic_index_in_dim(block, 1 - side, 0, False),
        )

    s1 = dot(own, own)
    s2, s2t = products(own_parts, a_parts)
    keep, send = zip(*(halves(s) for s in (s1, s2, s2t)))
    early = jnp.stack(keep) + move(jnp.stack(send), turn(lambda r, q: r, 1))
    early = lax.optimization_barrier(early)

    lone = group_index == 1
    held = [jnp.where(lone, there, here) for there, here in zip(p_parts, own_parts)]
    forth, back = products(held, b_parts)
    far = jnp.where(lone, forth, back)
    near = jnp.where(lone, back, forth)
    far_keep, far_send = halves(far)
    near_keep, near_send = halves(near)

    route = {0: 6, 1: 3, 2: 0, 3: 1, 4: 2, 5: 7, 6: 4, 7: 5}
    beside = {0: 1, 1: 0, 4: 5, 5: 4}
    x = move(pack(far_keep), turn(lambda r, q: route[r]))
    xf = move(pack(far_send), turn(lambda r, q: route[r], 1))
    y = move(pack(near_send), turn(lambda r, q: beside.get(r, r), 1))
    ez = move(jnp.concatenate([early[2], near_keep], 1), turn(lambda r, q: r - 1))
    x, xf, y, ez = lax.optimization_barrier((x, xf, y, ez))
    x = x + xf

    def quarter_of(which):
        def rows(v):
            return lax.dynamic_slice_in_dim(v, which * quarter, quarter, 0)

        def lanes(v):
            return jnp.where(which == 0, v[:, :width], v[:, width:])

        far_rows = lanes(x)
        beside_rows = lanes(y)
        found = {
            0: rows(early[0]),
            -1: rows(early[1]),
            1: rows(ez[:, :width]),
            2: far_rows,
            -3: far_rows,
            -2: rows(near_keep) + beside_rows,
            3: rows(ez[:, width:]) + beside_rows,
        }
        blocks = []
        for b in range(n):
            offset = sign * (b - pos)
            value = found[0]
            for d, v in found.items():
                value = jnp.where(offset == d, v, value) if d else value
            blocks.append(value)
        return jnp.concatenate(blocks, 1)

    sign = 1 - 2 * core
    return (quarter_of(core) + swap(quarter_of(1 - core))) / (cols * PG)


def from_behind(block, axis, distance):
    devices = range(lax.axis_size(axis))
    route = [((i - distance) % len(devices), i) for i in devices]
    return lax.ppermute(block, axis, route)


def from_partner(value, axis, bit):
    mask = 2**bit
    pairs = [(source, source ^ mask) for source in range(lax.axis_size(axis))]
    return lax.ppermute(value, axis, pairs)


def long_line(jacobian_tiles):
    local_block = jacobian_tiles[0]
    blk_width = local_block.shape[0]
    params_all = local_block.shape[1] * PG
    cycle_len = lax.axis_size("walker") // PG
    my_index = lax.axis_index("walker")
    cycle_pos = my_index // PG
    my_group = my_index % PG
    quarter = blk_width // PG

    def tile_with(moving):
        return lax.dot_general(
            local_block, moving, (((1,), (1,)), ((), ())), preferred_element_type=jnp.float32
        )

    stack_init = jnp.zeros((cycle_len, blk_width, blk_width), jnp.float32)
    stack_init = lax.dynamic_update_index_in_dim(stack_init, tile_with(local_block), 0, 0)

    def advance(step_num, carried):
        moving, tile_stack = carried
        moving = from_behind(moving, "walker", -PG)
        tile_stack = lax.dynamic_update_index_in_dim(tile_stack, tile_with(moving), step_num, 0)
        return (moving, tile_stack)

    _, row_stack = lax.fori_loop(1, cycle_len, advance, (local_block, stack_init))
    for bit_num in range(PG.bit_length() - 2, -1, -1):
        half_rows = row_stack.shape[1] // 2
        my_bit = my_group >> bit_num & 1
        kept_rows = lax.dynamic_slice_in_dim(row_stack, my_bit * half_rows, half_rows, 1)
        sent_rows = lax.dynamic_slice_in_dim(row_stack, (1 - my_bit) * half_rows, half_rows, 1)
        row_stack = kept_rows + from_partner(sent_rows, "walker", bit_num)
    row_stack = jnp.roll(row_stack, cycle_pos, axis=0)
    gram_rows = jnp.transpose(row_stack, (1, 0, 2)).reshape(quarter, cycle_len * blk_width)
    return gram_rows / params_all


SPAN = 4
CUTS = (6, 14, 16)


def solution(mesh):
    meets = mesh.shape["walker"] == SPAN * PG
    return jax.shard_map(
        line if meets else long_line,
        mesh=mesh,
        in_specs=(P(("groups", "walker"), None, None),),
        out_specs=P(("groups", "walker"), None),
        check_vma=False,
    )
```
